32 devices in a mesh: ctx: 16 (over z, x, core), tp: 2 (over y).
Axes of the slice: x: 2, y: 2, z: 4, core: 2. Of those that a mesh axis runs over, the one named last changes fastest.
Arguments:
- queries: bfloat16 [16384, 4096], P('ctx', 'tp'), may hold values from -96 to 96
- rotated_key_rows: bfloat16 [16384, 2048], P('ctx', 'tp'), may hold values from -5 to 5
- value_head_rows: bfloat16 [16384, 2048], P('ctx', 'tp'), may hold values from -5 to 5
- w_out: bfloat16 [16, 256, 3840], P('tp', 'ctx'), may hold values from -0.09375 to 0.09375
- post_gain: float32 [3840], replicated, may hold values from 0.25 to 1.75
- doc_lengths: int32 [16], replicated, may hold values from 1 to 4096, 16384 in all
Outputs:
- normed_out: bfloat16 [16384, 3840], P(('ctx', 'tp'))
The draws below stay inside these ranges and needn't reach their ends.
All inputs are finite; a program needn't handle non-finite values.
Results may differ from the reference program's by a relative error of at most 0.0085.
Values may be sent and summed in bfloat16 or wider, within the bound.
No kernel may reach another device: no remote copies, remote signals or barrier semaphores. Data moves between devices by JAX's collectives and lax.ppermute only.
A program may use at most 192 MiB of HBM per device.

```python
import math
import jax
import jax.numpy as jnp
import numpy as np
from jax import lax

D = 3840
QUERY_HEADS = 16
KEY_VALUE_HEADS = 8
HEAD_SIZE = 256
ATTEND_WINDOW = 1024
DOCS = 16
SEQUENCE_TOKENS = 16384
N_TP = 2


def drawn_pair(key):
    key_portion = jnp.clip(jax.random.normal(jax.random.fold_in(key, 11), (SEQUENCE_TOKENS, KEY_VALUE_HEADS, HEAD_SIZE), jnp.float32), -4.5, 4.5)
    query_portion = jnp.clip(jax.random.normal(jax.random.fold_in(key, 12), (SEQUENCE_TOKENS, QUERY_HEADS, HEAD_SIZE), jnp.float32), -4.5, 4.5)
    return (query_portion.reshape(SEQUENCE_TOKENS, QUERY_HEADS * HEAD_SIZE), key_portion.reshape(SEQUENCE_TOKENS, KEY_VALUE_HEADS * HEAD_SIZE))


def draw_queries(key, part):
    return drawn_pair(key)[0].astype(jnp.bfloat16)


def draw_rotated_key_rows(key, part):
    return drawn_pair(key)[1].astype(jnp.bfloat16)


def level_of(rng, shape, pieces, least, top_value):
    level = 1.0
    for dim, shards_of in pieces:
        draws = jax.random.uniform(jax.random.fold_in(jax.random.fold_in(rng, 6), dim), (shards_of,), jnp.float32, least / len(pieces), top_value / len(pieces))
        level = level * jnp.repeat(jnp.exp(draws), shape[dim] // shards_of).reshape((-1,) + (1,) * (len(shape) - 1 - dim))
    return level


def profile(number_of, total, reach, skew):
    loads = [(1 << 20) // math.isqrt(rank ** skew) + 1 for rank in range(2, number_of + 1)]
    spare, holding = total - reach - (number_of - 1), [1] * (number_of - 1)
    while spare > 0:
        candidates = [i for i in range(number_of - 1) if holding[i] < reach]
        whole, left = sum([loads[i] for i in candidates]), spare
        for i in candidates:
            more = min(reach - holding[i], max(1, left * loads[i] // whole), spare)
            holding[i] = holding[i] + more
            spare = spare - more
    return np.array([reach] + holding)


def uneven_parts(key, amount, total, most, slope):
    if amount == 2:
        one = jax.random.randint(key, (), max(1, total - most), min(most, total - 1) + 1)
        return jnp.stack([one, total - one])
    lengths = jnp.asarray(profile(amount, total, most, slope), jnp.int32)
    twos = (amount - 1) // 2
    giver, sink = lengths[1:1 + 2 * twos:2], lengths[2:2 + 2 * twos:2]
    margin = jnp.minimum(giver - 1, most - sink)
    shifted = jax.random.randint(jax.random.fold_in(key, 1), (twos,), 0, 1 << 20) % (margin + 1)
    lengths = lengths.at[1:1 + 2 * twos:2].set(giver - shifted).at[2:2 + 2 * twos:2].set(sink + shifted)
    return lengths[jax.random.permutation(jax.random.fold_in(key, 2), amount)]


def bell_draw(own_key, dims, scale, bound, shards=(), kind=jnp.bfloat16):
    loudness = level_of(own_key, dims, shards, -0.22, 0.18) if shards else 1.0
    values = jax.random.normal(own_key, dims, jnp.float32) * scale * loudness
    return jnp.minimum(jnp.maximum(values, -bound), bound).astype(kind)


def setup_inputs(seed: int = 0) -> dict:
    arg_keys = jax.random.split(jax.random.key(seed), 7)
    return {
        "queries": draw_queries(jax.random.fold_in(arg_keys[6], 71), 0),
        "rotated_key_rows": draw_rotated_key_rows(jax.random.fold_in(arg_keys[6], 71), 0),
        "value_head_rows": bell_draw(arg_keys[2], (SEQUENCE_TOKENS, KEY_VALUE_HEADS * HEAD_SIZE), 1.0, 5.0, ((0, 16), (1, 2))),
        "w_out": bell_draw(arg_keys[3], (QUERY_HEADS, HEAD_SIZE, D), (QUERY_HEADS * HEAD_SIZE) ** -0.5, 0.09375, ((0, 2), (1, 16))),
        "post_gain": jnp.clip(1.0 + 0.15 * jax.random.normal(arg_keys[4], (D,), jnp.float32), 0.25, 1.75),
        "doc_lengths": uneven_parts(arg_keys[5], DOCS, SEQUENCE_TOKENS, SEQUENCE_TOKENS // 4, 2).astype(jnp.int32),
    }


def post_norm(summed, post_gain):
    mean_sq = lax.optimization_barrier(jnp.mean(summed * summed, axis=-1, keepdims=True))
    return (summed * lax.rsqrt(mean_sq + 1e-06) * post_gain).astype(jnp.bfloat16)

def reference(queries, rotated_key_rows, value_head_rows, w_out, post_gain, doc_lengths):
    head_groups = QUERY_HEADS // KEY_VALUE_HEADS
    scaling = HEAD_SIZE ** (-0.5)
    doc_ends = jnp.cumsum(doc_lengths).astype(jnp.int32)
    positions = jnp.arange(SEQUENCE_TOKENS, dtype=jnp.int32)
    doc_of = lax.optimization_barrier(jnp.sum((doc_ends[None, :] <= positions[:, None]).astype(jnp.int32), axis=1))
    padded_keys = jnp.concatenate([jnp.zeros((ATTEND_WINDOW, KEY_VALUE_HEADS * HEAD_SIZE), jnp.bfloat16), rotated_key_rows], axis=0)
    padded_values = jnp.concatenate([jnp.zeros((ATTEND_WINDOW, KEY_VALUE_HEADS * HEAD_SIZE), jnp.bfloat16), value_head_rows], axis=0)
    kpos_pad = jnp.concatenate([jnp.arange(-ATTEND_WINDOW, 0, dtype=jnp.int32), positions])
    kdoc_pad = jnp.concatenate([jnp.full((ATTEND_WINDOW,), -1, jnp.int32), doc_of])
    query_block_size = min(512, SEQUENCE_TOKENS)
    key_block_size = ATTEND_WINDOW + query_block_size

    def one_block(block_id):
        block_start = (block_id * query_block_size).astype(jnp.int32)
        query_block = lax.dynamic_slice_in_dim(queries, block_start, query_block_size, 0).reshape(query_block_size, KEY_VALUE_HEADS, head_groups, HEAD_SIZE)
        key_block = lax.dynamic_slice_in_dim(padded_keys, block_start, key_block_size, 0).reshape(key_block_size, KEY_VALUE_HEADS, HEAD_SIZE)
        value_block = lax.dynamic_slice_in_dim(padded_values, block_start, key_block_size, 0).reshape(key_block_size, KEY_VALUE_HEADS, HEAD_SIZE)
        qpos = block_start + jnp.arange(query_block_size, dtype=jnp.int32)
        kpos = lax.dynamic_slice_in_dim(kpos_pad, block_start, key_block_size, 0)
        qdoc = lax.dynamic_slice_in_dim(doc_of, block_start, query_block_size, 0)
        kdoc = lax.dynamic_slice_in_dim(kdoc_pad, block_start, key_block_size, 0)
        allowed = (kpos[None, :] >= 0) & (kpos[None, :] <= qpos[:, None]) & (qpos[:, None] - kpos[None, :] < ATTEND_WINDOW) & (kdoc[None, :] == qdoc[:, None])
        scores = jnp.einsum('qhgd,khd->hgqk', query_block.astype(jnp.float32), key_block.astype(jnp.float32)) * scaling
        scores = jnp.where(allowed[None, None], scores, -jnp.inf)
        top = lax.optimization_barrier(jnp.max(scores, axis=-1, keepdims=True))
        expo = jnp.exp(scores - top)
        weights = (expo / lax.optimization_barrier(jnp.sum(expo, axis=-1, keepdims=True))).astype(jnp.bfloat16)
        result = jnp.einsum('hgqk,khd->qhgd', weights.astype(jnp.float32), value_block.astype(jnp.float32))
        return result.reshape(query_block_size, QUERY_HEADS * HEAD_SIZE).astype(jnp.bfloat16)
    attn = lax.map(one_block, jnp.arange(SEQUENCE_TOKENS // query_block_size, dtype=jnp.int32)).reshape(SEQUENCE_TOKENS, QUERY_HEADS * HEAD_SIZE)
    group_width = QUERY_HEADS // N_TP * HEAD_SIZE
    weight_groups = w_out.reshape(N_TP, group_width, D)

    def add_group(group_id, summed):
        cols = lax.dynamic_slice_in_dim(attn, (group_id * group_width).astype(jnp.int32), group_width, 1)
        partial_value = jnp.dot(cols, weight_groups[group_id], preferred_element_type=jnp.float32).astype(jnp.bfloat16)
        return summed + partial_value.astype(jnp.float32)
    summed = lax.fori_loop(0, N_TP, add_group, jnp.zeros((SEQUENCE_TOKENS, D), jnp.float32))
    return post_norm(summed, post_gain)
```

```python
import functools

import jax
import jax.numpy as jnp
from jax import lax
from jax.experimental import pallas as pl
from jax.experimental.pallas import tpu as pltpu
from jax.sharding import PartitionSpec as P

HEAD_SIZE = 256
ATTEND_WINDOW = 1024
MASKED = -1e30
LOG2E = 1.4426950408889634
EXP_SCALE = LOG2E * HEAD_SIZE ** (-0.5)
VMEM_BYTES = 56 << 20


def params(**kwargs):
    return pltpu.CompilerParams(vmem_limit_bytes=VMEM_BYTES, **kwargs)


def stacked_queries(q_ref, row, rows, groups):
    return jnp.concatenate(
        [q_ref[row : row + rows, h * HEAD_SIZE : (h + 1) * HEAD_SIZE] for h in range(groups)], axis=0
    )


def dot_nt(a, b):
    return lax.dot_general(a, b, (((1,), (1,)), ((), ())), preferred_element_type=jnp.float32)


def own_kernel(rows, groups, lo_ref, q_ref, k_ref, v_ref, acc_ref, stat_ref):
    tokens = q_ref.shape[0]
    for row in range(0, tokens, rows):
        keys = row + rows
        q = stacked_queries(q_ref, row, rows, groups)
        s = dot_nt(q, k_ref[:keys, :])
        lo = lo_ref[row : row + rows, :1]
        kpos = lax.broadcasted_iota(jnp.int32, (rows, keys), 1)
        qpos = row + lax.broadcasted_iota(jnp.int32, (rows, keys), 0)
        allowed = (kpos >= lo) & (kpos <= qpos)
        lane = lax.broadcasted_iota(jnp.int32, (rows, 128), 1)
        stats = jnp.zeros((rows, 128), jnp.float32)
        for h in range(groups):
            sh = jnp.where(allowed, s[h * rows : (h + 1) * rows], MASKED)
            top = jnp.max(sh, axis=1, keepdims=True)
            p = jnp.exp2((sh - top) * EXP_SCALE)
            total = jnp.sum(p, axis=1, keepdims=True)
            acc_ref[row : row + rows, h * HEAD_SIZE : (h + 1) * HEAD_SIZE] = jnp.dot(
                p.astype(jnp.bfloat16), v_ref[:keys, :], preferred_element_type=jnp.float32
            )
            stats = jnp.where(lane == 2 * h, top, stats)
            stats = jnp.where(lane == 2 * h + 1, total, stats)
        stat_ref[row : row + rows, :] = stats


def halo_kernel(rows, groups, lo_ref, q_ref, k_ref, v_ref, acc_ref, stat_ref, out_ref):
    tokens = q_ref.shape[0]
    for row in range(0, tokens, rows):
        keys = ATTEND_WINDOW - row
        q = stacked_queries(q_ref, row, rows, groups)
        s = dot_nt(q, k_ref[row:, :])
        lo = lo_ref[row : row + rows, :1]
        kpos = row - ATTEND_WINDOW + lax.broadcasted_iota(jnp.int32, (rows, keys), 1)
        allowed = kpos >= lo
        for h in range(groups):
            cols = slice(h * HEAD_SIZE, (h + 1) * HEAD_SIZE)
            sh = jnp.where(allowed, s[h * rows : (h + 1) * rows], MASKED)
            top_own = stat_ref[row : row + rows, 2 * h : 2 * h + 1]
            total_own = stat_ref[row : row + rows, 2 * h + 1 : 2 * h + 2]
            top = jnp.maximum(jnp.max(sh, axis=1, keepdims=True), top_own)
            p = jnp.exp2((sh - top) * EXP_SCALE)
            fade = jnp.exp2((top_own - top) * EXP_SCALE)
            total = jnp.sum(p, axis=1, keepdims=True) + fade * total_own
            acc = acc_ref[row : row + rows, cols] * fade + jnp.dot(
                p.astype(jnp.bfloat16), v_ref[row:, :], preferred_element_type=jnp.float32
            )
            out_ref[row : row + rows, cols] = (acc / total).astype(jnp.bfloat16)


def attention_calls(tokens, heads, kv_heads):
    groups = heads // kv_heads
    rows = min(256, tokens)
    width = groups * HEAD_SIZE
    lo_spec = pl.BlockSpec((tokens, 128), lambda g: (0, 0))
    q_spec = pl.BlockSpec((tokens, width), lambda g: (0, g))
    kv_spec = pl.BlockSpec((tokens, HEAD_SIZE), lambda g: (0, g))
    stat_spec = pl.BlockSpec((tokens, 128), lambda g: (0, g))
    flops = 2 * heads * tokens * (tokens + rows) * HEAD_SIZE
    cost = pl.CostEstimate(
        flops=4 * flops, transcendentals=heads * tokens * tokens // 2, bytes_accessed=tokens * heads * HEAD_SIZE * 8
    )
    own = pl.pallas_call(
        functools.partial(own_kernel, rows, groups),
        grid=(kv_heads,),
        in_specs=[lo_spec, q_spec, kv_spec, kv_spec],
        out_specs=[q_spec, stat_spec],
        out_shape=[
            jax.ShapeDtypeStruct((tokens, heads * HEAD_SIZE), jnp.float32),
            jax.ShapeDtypeStruct((tokens, kv_heads * 128), jnp.float32),
        ],
        compiler_params=params(),
        cost_estimate=cost,
        name="attend_own",
    )
    halo = pl.pallas_call(
        functools.partial(halo_kernel, rows, groups),
        grid=(kv_heads,),
        in_specs=[lo_spec, q_spec, kv_spec, kv_spec, q_spec, stat_spec],
        out_specs=q_spec,
        out_shape=jax.ShapeDtypeStruct((tokens, heads * HEAD_SIZE), jnp.bfloat16),
        compiler_params=params(),
        cost_estimate=cost,
        name="attend_halo",
    )
    return own, halo


def project_kernel(pieces, piece_rows, rows, where_ref, attn_ref, *refs):
    piece_refs = refs[: len(pieces)]
    out_ref, attn_buf, w_buf, sem = refs[len(pieces) :]
    start = pl.multiple_of(where_ref[sum(pieces)], rows)
    copies = [pltpu.make_async_copy(attn_ref.at[pl.ds(start, rows), :], attn_buf, sem.at[0])]
    slot = 0
    for ref, count in zip(piece_refs, pieces):
        for i in range(count):
            at = pl.multiple_of(where_ref[slot] * piece_rows, piece_rows)
            copies.append(
                pltpu.make_async_copy(ref.at[i], w_buf.at[:, pl.ds(at, piece_rows), :], sem.at[slot + 1])
            )
            slot += 1
    for copy in copies:
        copy.start()
    for copy in copies:
        copy.wait()
    depth = w_buf.shape[0] * w_buf.shape[1]
    out_ref[...] = jnp.dot(
        attn_buf[...], w_buf[...].reshape(depth, w_buf.shape[2]), preferred_element_type=jnp.float32
    ).astype(jnp.bfloat16)


def project(where, attn, piece_arrays, rows, name):
    pieces = [a.shape[0] for a in piece_arrays]
    _, heads, piece_rows, columns = piece_arrays[0].shape
    depth = attn.shape[1]
    any_spec = pl.BlockSpec(memory_space=pl.ANY)
    return pl.pallas_call(
        functools.partial(project_kernel, pieces, piece_rows, rows),
        grid_spec=pltpu.PrefetchScalarGridSpec(
            num_scalar_prefetch=1,
            grid=(1,),
            in_specs=[any_spec] * (1 + len(pieces)),
            out_specs=pl.BlockSpec((rows, columns), lambda i, where: (0, 0)),
            scratch_shapes=[
                pltpu.VMEM((rows, depth), jnp.bfloat16),
                pltpu.VMEM((heads, HEAD_SIZE, columns), jnp.bfloat16),
                pltpu.SemaphoreType.DMA((sum(pieces) + 1,)),
            ],
        ),
        out_shape=jax.ShapeDtypeStruct((rows, columns), jnp.bfloat16),
        compiler_params=params(),
        cost_estimate=pl.CostEstimate(
            flops=2 * rows * depth * columns,
            transcendentals=0,
            bytes_accessed=2 * (rows * depth + depth * columns + rows * columns),
        ),
        name=name,
    )(where, attn, *piece_arrays)


def norm_kernel(chunks, gain_ref, *refs):
    out_ref = refs[-1]
    sums, square, column = [], 0.0, 0
    for i in range(chunks):
        total = refs[i][...].astype(jnp.float32) + refs[chunks + i][...].astype(jnp.float32)
        square = square + jnp.sum(total * total, axis=1, keepdims=True)
        sums.append(total)
    factor = lax.rsqrt(square / out_ref.shape[1] + 1e-06)
    for total in sums:
        width = total.shape[1]
        gain = gain_ref[:, column : column + width]
        out_ref[:, column : column + width] = (total * factor * gain).astype(jnp.bfloat16)
        column += width


def sum_and_norm(kept, arrived, post_gain):
    rows = kept[0].shape[0]
    block = min(64, rows)
    total = sum(a.shape[1] for a in kept)
    specs = [pl.BlockSpec((block, a.shape[1]), lambda i: (i, 0)) for a in kept + arrived]
    return pl.pallas_call(
        functools.partial(norm_kernel, len(kept)),
        grid=(rows // block,),
        in_specs=[pl.BlockSpec((1, total), lambda i: (0, 0))] + specs,
        out_specs=pl.BlockSpec((block, total), lambda i: (i, 0)),
        out_shape=jax.ShapeDtypeStruct((rows, total), jnp.bfloat16),
        compiler_params=params(),
        cost_estimate=pl.CostEstimate(flops=8 * rows * total, transcendentals=rows, bytes_accessed=6 * rows * total),
        name="sum_and_norm",
    )(post_gain.reshape(1, total), *kept, *arrived)


def ctx_pairs(size, move):
    pairs = []
    for i in range(size):
        target = move(i // 4, (i // 2) % 2, i % 2)
        if target is not None:
            pairs.append((i, target[0] * 4 + target[1] * 2 + target[2]))
    return pairs


class Gather:
    def __init__(self, size):
        self.x = ctx_pairs(size, lambda z, x, c: (z, 1 - x, c))
        self.core = ctx_pairs(size, lambda z, x, c: (z, x, 1 - c))
        self.z1 = ctx_pairs(size, lambda z, x, c: (z ^ 1, x, c))
        self.z2 = ctx_pairs(size, lambda z, x, c: (3 - z, x, c) if z in (1, 2) else None)
        self.z3 = ctx_pairs(size, lambda z, x, c: (0 if z == 1 else 3, x, c) if z in (1, 2) else None)

    def send(self, array, pairs):
        return lax.ppermute(array, "ctx", pairs)

    def along_z(self, array, edge):
        near = self.send(array, self.z1)
        both = jnp.concatenate([array, near], axis=0)
        far = self.send(both, self.z2)
        passed = self.send(far, self.z3)
        return jnp.concatenate([both, jnp.where(edge, passed, far)], axis=0)

    def pieces(self, array, edge, x_first):
        if x_first:
            array = jnp.concatenate([array, self.send(array, self.x)], axis=0)
            array = self.along_z(array, edge)
        else:
            array = self.along_z(array, edge)
            array = jnp.concatenate([array, self.send(array, self.x)], axis=0)
        return [array, self.send(array, self.core)]

    def order(self, index, x_first):
        z, x, core = index // 4, (index // 2) % 2, index % 2
        far = jnp.where(z < 2, 2, 1)
        last = jnp.where(z < 2, 3, 0)
        zs = [z, z ^ 1, far, last]
        if x_first:
            places = [zz * 4 + xx * 2 for zz in zs for xx in (x, 1 - x)]
        else:
            places = [zz * 4 + xx * 2 for xx in (x, 1 - x) for zz in zs]
        return [p + core for p in places] + [p + 1 - core for p in places]


CHUNKS = ((768, True), (768, False), (768, True), (768, False), (768, False))


def on_device(queries, rotated_key_rows, value_head_rows, w_out, post_gain, doc_lengths):
    tokens = queries.shape[0]
    heads = queries.shape[1] // HEAD_SIZE
    kv_heads = rotated_key_rows.shape[1] // HEAD_SIZE
    ctx_size, tp_size = lax.axis_size("ctx"), lax.axis_size("tp")
    ctx_index, tp_index = lax.axis_index("ctx"), lax.axis_index("tp")
    grid_gather = ctx_size == 16

    forward = [(i, i + 1) for i in range(ctx_size - 1)]
    halo_keys = lax.ppermute(rotated_key_rows, "ctx", forward)
    halo_vals = lax.ppermute(value_head_rows, "ctx", forward)

    position = ctx_index * tokens + jnp.arange(tokens, dtype=jnp.int32)
    doc_ends = jnp.cumsum(doc_lengths)
    ended = doc_ends[None, :] <= position[:, None]
    doc_start = jnp.max(jnp.where(ended, doc_ends[None, :], 0), axis=1)
    low = jnp.maximum(position - (ATTEND_WINDOW - 1), doc_start) - ctx_index * tokens
    low = jnp.broadcast_to(low[:, None], (tokens, 128))

    attend_own, attend_halo = attention_calls(tokens, heads, kv_heads)
    acc, stats = attend_own(low, queries, rotated_key_rows, value_head_rows)
    attn = attend_halo(low, queries, halo_keys, halo_vals, acc, stats)

    rows = tokens // tp_size
    chunk_plan = CHUNKS if sum(c for c, _ in CHUNKS) == w_out.shape[2] else ((w_out.shape[2], False),)
    gather = Gather(ctx_size)
    kept, arrived = [], []
    column = 0
    for number, (width, x_first) in enumerate(chunk_plan):
        part = w_out[:, :, column : column + width]
        column += width
        if grid_gather:
            z = ctx_index // 4
            pieces = gather.pieces(part[None], (z == 0) | (z == 3), x_first)
            order = gather.order(ctx_index, x_first)
        else:
            pieces = [lax.all_gather(part, "ctx", axis=0, tiled=False)]
            order = list(range(ctx_size))
        order = [jnp.asarray(o, jnp.int32) for o in order]
        if tp_size == 2:
            send_at = jnp.stack(order + [((1 - tp_index) * rows).astype(jnp.int32)])
            keep_at = jnp.stack(order + [(tp_index * rows).astype(jnp.int32)])
            send = project(send_at, attn, pieces, rows, f"project_send{number}")
            arrived.append(lax.ppermute(send, "tp", [(0, 1), (1, 0)]))
            kept.append(project(keep_at, attn, pieces, rows, f"project_keep{number}"))
        else:
            all_at = jnp.stack(order + [jnp.asarray(0, jnp.int32)])
            partial = project(all_at, attn, pieces, tokens, f"project{number}")
            mine = lax.psum_scatter(partial, "tp", scatter_dimension=0, tiled=True)
            kept.append(mine)
            arrived.append(jnp.zeros_like(mine))
    return sum_and_norm(kept, arrived, post_gain)


def solution(mesh):
    placed = (P("ctx", "tp"), P("ctx", "tp"), P("ctx", "tp"), P("tp", "ctx", None), P(), P())
    return jax.shard_map(
        on_device, mesh=mesh, in_specs=placed, out_specs=P(("ctx", "tp"), None), check_vma=False
    )
```

```python
import functools

import jax
import jax.numpy as jnp
from jax import lax
from jax.experimental import pallas as pl
from jax.experimental.pallas import tpu as pltpu
from jax.sharding import PartitionSpec as P

HEAD_SIZE = 256
ATTEND_WINDOW = 1024
MASKED = -1e30
LOG2E = 1.4426950408889634
EXP_SCALE = LOG2E * HEAD_SIZE ** (-0.5)
VMEM_BYTES = 56 << 20
BRIEF = pl.CostEstimate(flops=1, transcendentals=0, bytes_accessed=1)


def params(**kwargs):
    return pltpu.CompilerParams(vmem_limit_bytes=VMEM_BYTES, **kwargs)


def stacked_queries(q_ref, row, rows, groups):
    return jnp.concatenate(
        [q_ref[row : row + rows, h * HEAD_SIZE : (h + 1) * HEAD_SIZE] for h in range(groups)], axis=0
    )


def dot_nt(a, b):
    return lax.dot_general(a, b, (((1,), (1,)), ((), ())), preferred_element_type=jnp.float32)


def attend_kernel(rows, groups, lo_ref, q_ref, k_ref, v_ref, halo_ref, out_ref):
    tokens = q_ref.shape[0]
    for row in range(0, tokens, rows):
        q = stacked_queries(q_ref, row, rows, groups)
        lo = lo_ref[row : row + rows, :1]
        spans = [(halo_ref[row:, :HEAD_SIZE], halo_ref[row:, HEAD_SIZE:], row - ATTEND_WINDOW)]
        if row:
            spans.append((k_ref[:row, :], v_ref[:row, :], 0))
        spans.append((k_ref[row : row + rows, :], v_ref[row : row + rows, :], row))
        scores = []
        for keys, _, first in spans:
            s = dot_nt(q, keys)
            kpos = first + lax.broadcasted_iota(jnp.int32, (rows, s.shape[1]), 1)
            allowed = kpos >= lo
            if first == row:
                allowed &= kpos <= row + lax.broadcasted_iota(jnp.int32, (rows, s.shape[1]), 0)
            scores.append([jnp.where(allowed, s[h * rows : (h + 1) * rows], MASKED) for h in range(groups)])
        for h in range(groups):
            top = functools.reduce(jnp.maximum, [jnp.max(s[h], axis=1, keepdims=True) for s in scores])
            total, acc = 0.0, 0.0
            for s, (_, values, _) in zip(scores, spans):
                p = jnp.exp2((s[h] - top) * EXP_SCALE)
                total = total + jnp.sum(p, axis=1, keepdims=True)
                acc = acc + jnp.dot(p.astype(jnp.bfloat16), values, preferred_element_type=jnp.float32)
            out_ref[row : row + rows, h * HEAD_SIZE : (h + 1) * HEAD_SIZE] = (acc * (1.0 / total)).astype(jnp.bfloat16)


def attend(low, queries, keys, values, halo, head, groups):
    tokens = queries.shape[0]
    rows = min(256, tokens)
    width = groups * HEAD_SIZE
    kv_spec = pl.BlockSpec((tokens, HEAD_SIZE), lambda i: (0, head))
    return pl.pallas_call(
        functools.partial(attend_kernel, rows, groups),
        grid=(1,),
        in_specs=[
            pl.BlockSpec((tokens, 128), lambda i: (0, 0)),
            pl.BlockSpec((tokens, width), lambda i: (0, head)),
            kv_spec,
            kv_spec,
            pl.BlockSpec((tokens, 2 * HEAD_SIZE), lambda i: (0, 0)),
        ],
        out_specs=pl.BlockSpec((tokens, width), lambda i: (0, 0)),
        out_shape=jax.ShapeDtypeStruct((tokens, width), jnp.bfloat16),
        compiler_params=params(),
        cost_estimate=BRIEF,
        name=f"attend{head}",
    )(low, queries, keys, values, halo)


def project_kernel(parts, column, outs, where_ref, *refs):
    attn_refs, refs = refs[:parts], refs[parts:]
    blocks_ref, refs = refs[0], refs[1:]
    out_refs, (attn_buf, w_buf, sem, attn_sem) = refs[:outs], refs[outs:]
    blocks, heads, block_rows, _ = blocks_ref.shape
    columns = w_buf.shape[2]
    cuts = [0, columns // 256 * 128, columns]
    w_copies = []
    for half in range(2):
        span = slice(cuts[half], cuts[half + 1])
        source = slice(column + cuts[half], column + cuts[half + 1])
        copies = []
        for i in range(blocks):
            at = pl.multiple_of(where_ref[i] * block_rows, block_rows)
            copies.append(
                pltpu.make_async_copy(
                    blocks_ref.at[i, :, :, source], w_buf.at[:, pl.ds(at, block_rows), span], sem.at[half, i]
                )
            )
        w_copies.append(copies)
    width = attn_buf.shape[2] // parts
    rows = attn_buf.shape[1]
    attn_copies = []
    for out in range(outs):
        start = pl.multiple_of(where_ref[blocks + out], rows)
        attn_copies.append(
            [
                pltpu.make_async_copy(
                    ref.at[pl.ds(start, rows), :], attn_buf.at[out, :, i * width : (i + 1) * width], attn_sem.at[out, i]
                )
                for i, ref in enumerate(attn_refs)
            ]
        )
    for copy in attn_copies[0] + w_copies[0] + w_copies[1] + sum(attn_copies[1:], []):
        copy.start()
    depth = heads * HEAD_SIZE
    for out in range(outs):
        for copy in attn_copies[out]:
            copy.wait()
        for half in range(2):
            if out == 0:
                for copy in w_copies[half]:
                    copy.wait()
            span = slice(cuts[half], cuts[half + 1])
            out_refs[out][:, span] = jnp.dot(
                attn_buf[out],
                w_buf[:, :, span].reshape(depth, cuts[half + 1] - cuts[half]),
                preferred_element_type=jnp.float32,
            ).astype(jnp.bfloat16)


def project(where, attn, blocks, column, columns, outs, name):
    count, heads, _, _ = blocks.shape
    rows = attn[0].shape[0] // outs
    depth = sum(a.shape[1] for a in attn)
    any_spec = pl.BlockSpec(memory_space=pl.ANY)
    return pl.pallas_call(
        functools.partial(project_kernel, len(attn), column, outs),
        grid_spec=pltpu.PrefetchScalarGridSpec(
            num_scalar_prefetch=1,
            grid=(1,),
            in_specs=[any_spec] * (len(attn) + 1),
            out_specs=[pl.BlockSpec((rows, columns), lambda i, where: (0, 0))] * outs,
            scratch_shapes=[
                pltpu.VMEM((outs, rows, depth), jnp.bfloat16),
                pltpu.VMEM((heads, HEAD_SIZE, columns), jnp.bfloat16),
                pltpu.SemaphoreType.DMA((2, count)),
                pltpu.SemaphoreType.DMA((outs, len(attn))),
            ],
        ),
        out_shape=[jax.ShapeDtypeStruct((rows, columns), jnp.bfloat16)] * outs,
        compiler_params=params(),
        cost_estimate=BRIEF,
        name=name,
    )(where, *attn, blocks)


def norm_kernel(chunks, gain_ref, *refs):
    out_ref = refs[-1]
    sums, square, column = [], 0.0, 0
    for i in range(chunks):
        total = refs[i][...].astype(jnp.float32) + refs[chunks + i][...].astype(jnp.float32)
        square = square + jnp.sum(total * total, axis=1, keepdims=True)
        sums.append(total)
    factor = lax.rsqrt(square / out_ref.shape[1] + 1e-06)
    for total in sums:
        width = total.shape[1]
        gain = gain_ref[:, column : column + width]
        out_ref[:, column : column + width] = (total * factor * gain).astype(jnp.bfloat16)
        column += width


def sum_and_norm(kept, arrived, post_gain):
    rows = kept[0].shape[0]
    block = min(128, rows)
    total = sum(a.shape[1] for a in kept)
    specs = [pl.BlockSpec((block, a.shape[1]), lambda i: (i, 0)) for a in kept + arrived]
    return pl.pallas_call(
        functools.partial(norm_kernel, len(kept)),
        grid=(rows // block,),
        in_specs=[pl.BlockSpec((1, total), lambda i: (0, 0))] + specs,
        out_specs=pl.BlockSpec((block, total), lambda i: (i, 0)),
        out_shape=jax.ShapeDtypeStruct((rows, total), jnp.bfloat16),
        compiler_params=params(),
        cost_estimate=BRIEF,
        name="sum_and_norm",
    )(post_gain.reshape(1, total), *kept, *arrived)


def ring_order(size):
    if size % 4:
        return list(range(size))
    up = [z * 4 + core for z in range(size // 4) for core in (0, 1)]
    down = [z * 4 + 2 + core for z in reversed(range(size // 4)) for core in (0, 1)]
    return up + down


def tie(values, after):
    if after is None:
        return values
    return lax.optimization_barrier((values, after))[0]


CHUNKS = ((1024, 896), (1024, 896))


def row_limits(ctx_index, tokens, doc_lengths):
    position = ctx_index * tokens + jnp.arange(tokens, dtype=jnp.int32)
    doc_ends = jnp.cumsum(doc_lengths)
    ended = doc_ends[None, :] <= position[:, None]
    doc_start = jnp.max(jnp.where(ended, doc_ends[None, :], 0), axis=1)
    low = jnp.maximum(position - (ATTEND_WINDOW - 1), doc_start) - ctx_index * tokens
    return jnp.broadcast_to(low[:, None], (tokens, 128))


def halo_of(keys, values, head, after=None):
    size = lax.axis_size("ctx")
    cols = slice(head * HEAD_SIZE, (head + 1) * HEAD_SIZE)
    both = tie(jnp.concatenate([keys[:, cols], values[:, cols]], axis=1), after)
    return lax.ppermute(both, "ctx", [(i, i + 1) for i in range(size - 1)])


def on_device(queries, rotated_key_rows, value_head_rows, w_out, post_gain, doc_lengths):
    tokens = queries.shape[0]
    heads = queries.shape[1] // HEAD_SIZE
    kv_heads = rotated_key_rows.shape[1] // HEAD_SIZE
    ctx_size, tp_size = lax.axis_size("ctx"), lax.axis_size("tp")
    tp_index = lax.axis_index("tp")
    rows = tokens // tp_size
    low = row_limits(lax.axis_index("ctx"), tokens, doc_lengths)

    halos = []
    for head in range(kv_heads):
        cols = slice(head * HEAD_SIZE, (head + 1) * HEAD_SIZE)
        both = jnp.concatenate([rotated_key_rows[:, cols], value_head_rows[:, cols]], axis=1)
        halos.append(lax.ppermute(both, "ctx", [(i, i + 1) for i in range(ctx_size - 1)]))
    ring = ring_order(ctx_size)
    gathered, column = [], 0
    for widths in CHUNKS:
        part = w_out[:, :, column : column + sum(widths)]
        gathered.append(lax.all_gather(part, "ctx", axis=0, tiled=False, axis_index_groups=[ring]))
        column += sum(widths)

    attn = []
    for head in range(kv_heads):
        after = (halos[head], attn[-1]) if attn else halos[head]
        attn.append(
            attend(tie(low, after), queries, rotated_key_rows, value_head_rows, halos[head], head, heads // kv_heads)
        )

    kept, arrived = [], []
    for gather, widths in zip(gathered, CHUNKS):
        column = 0
        for width in widths:
            number = len(kept)
            if tp_size == 2:
                starts = jnp.stack([(1 - tp_index) * rows, tp_index * rows])
                where = jnp.concatenate([jnp.array(ring, jnp.int32), starts.astype(jnp.int32)])
                if number >= 2:
                    where = tie(where, arrived[number - 2])
                send, keep = project(where, attn, gather, column, width, 2, f"project{number}")
                arrived.append(lax.ppermute(send, "tp", [(0, 1), (1, 0)]))
            else:
                where = jnp.array(ring + [0], jnp.int32)
                (keep,) = project(where, attn, gather, column, width, 1, f"project{number}")
                if tp_size > 1:
                    keep = lax.psum_scatter(keep, "tp", scatter_dimension=0, tiled=True)
                arrived.append(jnp.zeros_like(keep))
            kept.append(keep)
            column += width
    return sum_and_norm(kept, arrived, post_gain)


def solution(mesh):
    placed = (P("ctx", "tp"), P("ctx", "tp"), P("ctx", "tp"), P("tp", "ctx", None), P(), P())
    return jax.shard_map(
        on_device, mesh=mesh, in_specs=placed, out_specs=P(("ctx", "tp"), None), check_vma=False
    )
```

```python
import functools

import jax
import jax.numpy as jnp
from jax import lax
from jax.experimental import pallas as pl
from jax.experimental.pallas import tpu as pltpu
from jax.sharding import PartitionSpec as P

HEAD_SIZE = 256
ATTEND_WINDOW = 1024
MASKED = -1e30
LOG2E = 1.4426950408889634
EXP_SCALE = LOG2E * HEAD_SIZE ** (-0.5)
VMEM_BYTES = 44 << 20
BRIEF = pl.CostEstimate(flops=1, transcendentals=0, bytes_accessed=1)


def params(**kwargs):
    return pltpu.CompilerParams(vmem_limit_bytes=VMEM_BYTES, **kwargs)


def stacked_queries(q_ref, row, rows, groups):
    return jnp.concatenate(
        [q_ref[row : row + rows, h * HEAD_SIZE : (h + 1) * HEAD_SIZE] for h in range(groups)], axis=0
    )


def dot_nt(a, b):
    return lax.dot_general(a, b, (((1,), (1,)), ((), ())), preferred_element_type=jnp.float32)


def attend_kernel(
    rows, groups, near_ref, lo_ref, q_hbm, k_hbm, v_hbm, chip_ref, link_ref, out_ref, q_ref, k_ref, v_ref, halo_ref, sem
):
    width = q_ref.shape[1]
    head = near_ref[1]
    key_cols = pl.ds(pl.multiple_of(head * HEAD_SIZE, HEAD_SIZE), HEAD_SIZE)
    query_cols = pl.ds(pl.multiple_of(head * width, width), width)
    copies = [
        pltpu.make_async_copy(q_hbm.at[:, query_cols], q_ref, sem.at[0]),
        pltpu.make_async_copy(k_hbm.at[:, key_cols], k_ref, sem.at[1]),
        pltpu.make_async_copy(v_hbm.at[:, key_cols], v_ref, sem.at[2]),
    ]
    for copy in copies:
        copy.start()

    @pl.when(near_ref[0] == 1)
    def _():
        pltpu.make_async_copy(chip_ref, halo_ref, sem.at[3]).start()

    @pl.when(near_ref[0] != 1)
    def _():
        pltpu.make_async_copy(link_ref, halo_ref, sem.at[3]).start()

    for copy in copies:
        copy.wait()
    pltpu.make_async_copy(chip_ref, halo_ref, sem.at[3]).wait()
    tokens = q_ref.shape[0]
    for row in range(0, tokens, rows):
        q = stacked_queries(q_ref, row, rows, groups)
        lo = lo_ref[row : row + rows, :1]
        spans = [(halo_ref[row:, :HEAD_SIZE], halo_ref[row:, HEAD_SIZE:], row - ATTEND_WINDOW)]
        if row:
            spans.append((k_ref[:row, :], v_ref[:row, :], 0))
        spans.append((k_ref[row : row + rows, :], v_ref[row : row + rows, :], row))
        scores = []
        for keys, _, first in spans:
            s = dot_nt(q, keys)
            kpos = first + lax.broadcasted_iota(jnp.int32, (rows, s.shape[1]), 1)
            allowed = kpos >= lo
            if first == row:
                allowed &= kpos <= row + lax.broadcasted_iota(jnp.int32, (rows, s.shape[1]), 0)
            scores.append([jnp.where(allowed, s[h * rows : (h + 1) * rows], MASKED) for h in range(groups)])
        for h in range(groups):
            top = functools.reduce(jnp.maximum, [jnp.max(s[h], axis=1, keepdims=True) for s in scores])
            total, acc = 0.0, 0.0
            for s, (_, values, _) in zip(scores, spans):
                p = jnp.exp2((s[h] - top) * EXP_SCALE)
                total = total + jnp.sum(p, axis=1, keepdims=True)
                acc = acc + jnp.dot(p.astype(jnp.bfloat16), values, preferred_element_type=jnp.float32)
            out_ref[row : row + rows, h * HEAD_SIZE : (h + 1) * HEAD_SIZE] = (acc * (1.0 / total)).astype(jnp.bfloat16)


def attend(near, low, queries, keys, values, halo, groups):
    tokens = queries.shape[0]
    rows = min(256, tokens)
    width = groups * HEAD_SIZE
    any_spec = pl.BlockSpec(memory_space=pl.ANY)
    vmem_spec = pl.BlockSpec(memory_space=pltpu.VMEM)
    return pl.pallas_call(
        functools.partial(attend_kernel, rows, groups),
        in_specs=[pl.BlockSpec(memory_space=pltpu.SMEM), vmem_spec] + [any_spec] * 5,
        out_specs=vmem_spec,
        scratch_shapes=[
            pltpu.VMEM((tokens, width), jnp.bfloat16),
            pltpu.VMEM((tokens, HEAD_SIZE), jnp.bfloat16),
            pltpu.VMEM((tokens, HEAD_SIZE), jnp.bfloat16),
            pltpu.VMEM((tokens, 2 * HEAD_SIZE), jnp.bfloat16),
            pltpu.SemaphoreType.DMA((4,)),
        ],
        out_shape=jax.ShapeDtypeStruct((tokens, width), jnp.bfloat16),
        compiler_params=params(),
        cost_estimate=BRIEF,
        name="attend",
    )(near, low, queries, keys, values, *halo)


def project_kernel(parts, chunk, outs, where_ref, *refs):
    attn_refs, refs = refs[:parts], refs[parts:]
    blocks_ref, refs = refs[0], refs[1:]
    out_refs, (w_buf, sem) = refs[:outs], refs[outs:]
    blocks, _, heads, block_rows, columns = blocks_ref.shape
    copies = []
    for i in range(blocks):
        at = pl.multiple_of(where_ref[i] * block_rows, block_rows)
        copies.append(
            pltpu.make_async_copy(blocks_ref.at[i, chunk], w_buf.at[:, pl.ds(at, block_rows), :], sem.at[i])
        )
    for copy in copies:
        copy.start()
    for copy in copies:
        copy.wait()
    part_heads = heads // parts
    for out in range(outs):
        rows = out_refs[out].shape[0]
        start = pl.multiple_of(where_ref[blocks + out], rows)
        total = 0.0
        for i, ref in enumerate(attn_refs):
            w = w_buf[i * part_heads : (i + 1) * part_heads].reshape(part_heads * HEAD_SIZE, columns)
            total = total + jnp.dot(ref[pl.ds(start, rows), :], w, preferred_element_type=jnp.float32)
        out_refs[out][...] = total.astype(jnp.bfloat16)


def project(where, attn, blocks, chunk, outs):
    count, _, heads, _, columns = blocks.shape
    rows = attn[0].shape[0] // outs
    vmem_spec = pl.BlockSpec(memory_space=pltpu.VMEM)
    return pl.pallas_call(
        functools.partial(project_kernel, len(attn), chunk, outs),
        in_specs=[pl.BlockSpec(memory_space=pltpu.SMEM)]
        + [vmem_spec] * len(attn)
        + [pl.BlockSpec(memory_space=pl.ANY)],
        out_specs=[vmem_spec] * outs,
        scratch_shapes=[
            pltpu.VMEM((heads, HEAD_SIZE, columns), jnp.bfloat16),
            pltpu.SemaphoreType.DMA((count,)),
        ],
        out_shape=[jax.ShapeDtypeStruct((rows, columns), jnp.bfloat16)] * outs,
        compiler_params=params(),
        cost_estimate=BRIEF,
        name="project",
    )(where, *attn, blocks)


def norm_kernel(chunks, gain_ref, *refs):
    out_ref = refs[-1]
    sums, square, column = [], 0.0, 0
    for i in range(chunks):
        total = refs[i][...].astype(jnp.float32) + refs[chunks + i][...].astype(jnp.float32)
        square = square + jnp.sum(total * total, axis=1, keepdims=True)
        sums.append(total)
    factor = lax.rsqrt(square / out_ref.shape[1] + 1e-06)
    for total in sums:
        width = total.shape[1]
        gain = gain_ref[:, column : column + width]
        out_ref[:, column : column + width] = (total * factor * gain).astype(jnp.bfloat16)
        column += width


def sum_and_norm(kept, arrived, post_gain):
    rows = kept[0].shape[0]
    block = min(128, rows)
    total = sum(a.shape[1] for a in kept)
    specs = [pl.BlockSpec((block, a.shape[1]), lambda i: (i, 0)) for a in kept + arrived]
    return pl.pallas_call(
        functools.partial(norm_kernel, len(kept)),
        grid=(rows // block,),
        in_specs=[pl.BlockSpec((1, total), lambda i: (0, 0))] + specs,
        out_specs=pl.BlockSpec((block, total), lambda i: (i, 0)),
        out_shape=jax.ShapeDtypeStruct((rows, total), jnp.bfloat16),
        compiler_params=params(),
        cost_estimate=BRIEF,
        name="sum_and_norm",
    )(post_gain.reshape(1, total), *kept, *arrived)


def ring_order(size):
    if size % 4:
        return list(range(size))
    up = [z * 4 + core for z in range(size // 4) for core in (0, 1)]
    down = [z * 4 + 2 + core for z in reversed(range(size // 4)) for core in (0, 1)]
    return up + down


def tie(values, after):
    if after is None:
        return values
    return lax.optimization_barrier((values, after))[0]


CHUNKS = ((3, 768), (2, 768))


def row_limits(ctx_index, tokens, doc_lengths):
    position = ctx_index * tokens + jnp.arange(tokens, dtype=jnp.int32)
    doc_ends = jnp.cumsum(doc_lengths)
    ended = doc_ends[None, :] <= position[:, None]
    doc_start = jnp.max(jnp.where(ended, doc_ends[None, :], 0), axis=1)
    low = jnp.maximum(position - (ATTEND_WINDOW - 1), doc_start) - ctx_index * tokens
    return jnp.broadcast_to(low[:, None], (tokens, 128))


def on_device(queries, rotated_key_rows, value_head_rows, w_out, post_gain, doc_lengths):
    tokens = queries.shape[0]
    heads = queries.shape[1] // HEAD_SIZE
    kv_heads = rotated_key_rows.shape[1] // HEAD_SIZE
    ctx_size, tp_size = lax.axis_size("ctx"), lax.axis_size("tp")
    tp_index = lax.axis_index("tp")
    rows = tokens // tp_size
    low = row_limits(lax.axis_index("ctx"), tokens, doc_lengths)

    near = (lax.axis_index("ctx") % 2).astype(jnp.int32)
    halos = []
    for head in range(kv_heads):
        cols = slice(head * HEAD_SIZE, (head + 1) * HEAD_SIZE)
        both = jnp.concatenate([rotated_key_rows[:, cols], value_head_rows[:, cols]], axis=1)
        chip = lax.ppermute(both, "ctx", [(i, i ^ 1) for i in range(ctx_size)])
        link = lax.ppermute(chip, "ctx", [(i, i + 2) for i in range(0, ctx_size - 2, 2)])
        halos.append((chip, link))

    attn = []
    for head in range(kv_heads):
        after = (halos[head], attn[-1]) if attn else halos[head]
        which = jnp.stack([near, jnp.int32(head)])
        attn.append(
            attend(which, tie(low, after), queries, rotated_key_rows, value_head_rows, halos[head], heads // kv_heads)
        )

    ring = ring_order(ctx_size)
    gathered, column = [], 0
    for chunks, width in CHUNKS:
        part = jnp.stack([w_out[:, :, column + i * width : column + (i + 1) * width] for i in range(chunks)])
        if len(gathered) == 1:
            part = tie(part, (attn[:-1], [link for _, link in halos]))
        gathered.append(lax.all_gather(part, "ctx", axis=0, tiled=False, axis_index_groups=[ring]))
        column += chunks * width

    kept, arrived = [], []
    starts = [(1 - tp_index) * rows, tp_index * rows] if tp_size == 2 else [jnp.int32(0)]
    where = jnp.stack([jnp.int32(i) for i in ring] + [i.astype(jnp.int32) for i in starts])
    for gather in gathered:
        for chunk in range(gather.shape[1]):
            number = len(kept)
            if number:
                where = tie(where, (kept[-1], arrived[max(number - 2, 0)] if number > 1 else ()))
            if tp_size == 2:
                send, keep = project(where, attn, gather, chunk, 2)
                arrived.append(lax.ppermute(send, "tp", [(0, 1), (1, 0)]))
            else:
                (keep,) = project(where, attn, gather, chunk, 1)
                if tp_size > 1:
                    keep = lax.psum_scatter(keep, "tp", scatter_dimension=0, tiled=True)
                arrived.append(jnp.zeros_like(keep))
            kept.append(keep)
    return sum_and_norm(kept, arrived, post_gain)


def solution(mesh):
    placed = (P("ctx", "tp"), P("ctx", "tp"), P("ctx", "tp"), P("tp", "ctx", None), P(), P())
    return jax.shard_map(
        on_device, mesh=mesh, in_specs=placed, out_specs=P(("ctx", "tp"), None), check_vma=False
    )
```

```python
import functools

import jax
import jax.numpy as jnp
from jax import lax
from jax.experimental import pallas as pl
from jax.experimental.pallas import tpu as pltpu
from jax.sharding import PartitionSpec as P

HEAD_SIZE = 256
ATTEND_WINDOW = 1024
MASKED = -1e30
LOG2E = 1.4426950408889634
EXP_SCALE = LOG2E * HEAD_SIZE ** (-0.5)
VMEM_BYTES = 44 << 20
BRIEF = pl.CostEstimate(flops=1, transcendentals=0, bytes_accessed=1)


def params(**kwargs):
    return pltpu.CompilerParams(vmem_limit_bytes=VMEM_BYTES, **kwargs)


def stacked_queries(q_ref, row, rows, groups):
    return jnp.concatenate(
        [q_ref[row : row + rows, h * HEAD_SIZE : (h + 1) * HEAD_SIZE] for h in range(groups)], axis=0
    )


def dot_nt(a, b):
    return lax.dot_general(a, b, (((1,), (1,)), ((), ())), preferred_element_type=jnp.float32)


def attend_kernel(
    rows, groups, near_ref, lo_ref, q_hbm, k_hbm, v_hbm, chip_ref, link_ref, out_ref, q_ref, k_ref, v_ref, halo_ref, sem
):
    width = q_ref.shape[1]
    head = near_ref[1]
    key_cols = pl.ds(pl.multiple_of(head * HEAD_SIZE, HEAD_SIZE), HEAD_SIZE)
    query_cols = pl.ds(pl.multiple_of(head * width, width), width)
    copies = [
        pltpu.make_async_copy(q_hbm.at[:, query_cols], q_ref, sem.at[0]),
        pltpu.make_async_copy(k_hbm.at[:, key_cols], k_ref, sem.at[1]),
        pltpu.make_async_copy(v_hbm.at[:, key_cols], v_ref, sem.at[2]),
    ]
    for copy in copies:
        copy.start()

    @pl.when(near_ref[0] == 1)
    def _():
        pltpu.make_async_copy(chip_ref, halo_ref, sem.at[3]).start()

    @pl.when(near_ref[0] != 1)
    def _():
        pltpu.make_async_copy(link_ref, halo_ref, sem.at[3]).start()

    for copy in copies:
        copy.wait()
    pltpu.make_async_copy(chip_ref, halo_ref, sem.at[3]).wait()
    tokens = q_ref.shape[0]
    for row in range(0, tokens, rows):
        q = stacked_queries(q_ref, row, rows, groups)
        lo = lo_ref[row : row + rows, :1]
        spans = [(halo_ref[row:, :HEAD_SIZE], halo_ref[row:, HEAD_SIZE:], row - ATTEND_WINDOW)]
        if row:
            spans.append((k_ref[:row, :], v_ref[:row, :], 0))
        spans.append((k_ref[row : row + rows, :], v_ref[row : row + rows, :], row))
        scores = []
        for keys, _, first in spans:
            s = dot_nt(q, keys)
            kpos = first + lax.broadcasted_iota(jnp.int32, (rows, s.shape[1]), 1)
            allowed = kpos >= lo
            if first == row:
                allowed &= kpos <= row + lax.broadcasted_iota(jnp.int32, (rows, s.shape[1]), 0)
            scores.append([jnp.where(allowed, s[h * rows : (h + 1) * rows], MASKED) for h in range(groups)])
        for h in range(groups):
            top = functools.reduce(jnp.maximum, [jnp.max(s[h], axis=1, keepdims=True) for s in scores])
            total, acc = 0.0, 0.0
            for s, (_, values, _) in zip(scores, spans):
                p = jnp.exp2((s[h] - top) * EXP_SCALE)
                total = total + jnp.sum(p, axis=1, keepdims=True)
                acc = acc + jnp.dot(p.astype(jnp.bfloat16), values, preferred_element_type=jnp.float32)
            out_ref[row : row + rows, h * HEAD_SIZE : (h + 1) * HEAD_SIZE] = (acc * (1.0 / total)).astype(jnp.bfloat16)


def attend(near, low, queries, keys, values, halo, groups):
    tokens = queries.shape[0]
    rows = min(256, tokens)
    width = groups * HEAD_SIZE
    any_spec = pl.BlockSpec(memory_space=pl.ANY)
    vmem_spec = pl.BlockSpec(memory_space=pltpu.VMEM)
    return pl.pallas_call(
        functools.partial(attend_kernel, rows, groups),
        in_specs=[pl.BlockSpec(memory_space=pltpu.SMEM), vmem_spec] + [any_spec] * 5,
        out_specs=vmem_spec,
        scratch_shapes=[
            pltpu.VMEM((tokens, width), jnp.bfloat16),
            pltpu.VMEM((tokens, HEAD_SIZE), jnp.bfloat16),
            pltpu.VMEM((tokens, HEAD_SIZE), jnp.bfloat16),
            pltpu.VMEM((tokens, 2 * HEAD_SIZE), jnp.bfloat16),
            pltpu.SemaphoreType.DMA((4,)),
        ],
        out_shape=jax.ShapeDtypeStruct((tokens, width), jnp.bfloat16),
        compiler_params=params(),
        cost_estimate=BRIEF,
        name="attend",
    )(near, low, queries, keys, values, *halo)


def project_kernel(parts, chunk, outs, where_ref, *refs):
    attn_refs, refs = refs[:parts], refs[parts:]
    blocks_ref, refs = refs[0], refs[1:]
    out_refs, (w_buf, sem) = refs[:outs], refs[outs:]
    blocks, _, heads, block_rows, columns = blocks_ref.shape
    copies = []
    for i in range(blocks):
        at = pl.multiple_of(where_ref[i] * block_rows, block_rows)
        copies.append(
            pltpu.make_async_copy(blocks_ref.at[i, chunk], w_buf.at[:, pl.ds(at, block_rows), :], sem.at[i])
        )
    for copy in copies:
        copy.start()
    for copy in copies:
        copy.wait()
    part_heads = heads // parts
    for out in range(outs):
        rows = out_refs[out].shape[0]
        start = pl.multiple_of(where_ref[blocks + out], rows)
        total = 0.0
        for i, ref in enumerate(attn_refs):
            w = w_buf[i * part_heads : (i + 1) * part_heads].reshape(part_heads * HEAD_SIZE, columns)
            total = total + jnp.dot(ref[pl.ds(start, rows), :], w, preferred_element_type=jnp.float32)
        out_refs[out][...] = total.astype(jnp.bfloat16)


def project(where, attn, blocks, chunk, outs):
    count, _, heads, _, columns = blocks.shape
    rows = attn[0].shape[0] // outs
    vmem_spec = pl.BlockSpec(memory_space=pltpu.VMEM)
    return pl.pallas_call(
        functools.partial(project_kernel, len(attn), chunk, outs),
        in_specs=[pl.BlockSpec(memory_space=pltpu.SMEM)]
        + [vmem_spec] * len(attn)
        + [pl.BlockSpec(memory_space=pl.ANY)],
        out_specs=[vmem_spec] * outs,
        scratch_shapes=[
            pltpu.VMEM((heads, HEAD_SIZE, columns), jnp.bfloat16),
            pltpu.SemaphoreType.DMA((count,)),
        ],
        out_shape=[jax.ShapeDtypeStruct((rows, columns), jnp.bfloat16)] * outs,
        compiler_params=params(),
        cost_estimate=BRIEF,
        name="project",
    )(where, *attn, blocks)


def norm_kernel(chunks, gain_ref, *refs):
    out_ref = refs[-1]
    sums, square, column = [], 0.0, 0
    for i in range(chunks):
        total = refs[i][...].astype(jnp.float32) + refs[chunks + i][...].astype(jnp.float32)
        square = square + jnp.sum(total * total, axis=1, keepdims=True)
        sums.append(total)
    factor = lax.rsqrt(square / out_ref.shape[1] + 1e-06)
    for total in sums:
        width = total.shape[1]
        gain = gain_ref[:, column : column + width]
        out_ref[:, column : column + width] = (total * factor * gain).astype(jnp.bfloat16)
        column += width


def sum_and_norm(kept, arrived, post_gain):
    rows = kept[0].shape[0]
    block = min(128, rows)
    total = sum(a.shape[1] for a in kept)
    specs = [pl.BlockSpec((block, a.shape[1]), lambda i: (i, 0)) for a in kept + arrived]
    return pl.pallas_call(
        functools.partial(norm_kernel, len(kept)),
        grid=(rows // block,),
        in_specs=[pl.BlockSpec((1, total), lambda i: (0, 0))] + specs,
        out_specs=pl.BlockSpec((block, total), lambda i: (i, 0)),
        out_shape=jax.ShapeDtypeStruct((rows, total), jnp.bfloat16),
        compiler_params=params(),
        cost_estimate=BRIEF,
        name="sum_and_norm",
    )(post_gain.reshape(1, total), *kept, *arrived)


def ring_order(size):
    if size % 4:
        return list(range(size))
    up = [z * 4 + core for z in range(size // 4) for core in (0, 1)]
    down = [z * 4 + 2 + core for z in reversed(range(size // 4)) for core in (0, 1)]
    return up + down


def tie(values, after):
    if after is None:
        return values
    return lax.optimization_barrier((values, after))[0]


CHUNKS = ((3, 768), (2, 768))


def row_limits(ctx_index, tokens, doc_lengths):
    position = ctx_index * tokens + jnp.arange(tokens, dtype=jnp.int32)
    doc_ends = jnp.cumsum(doc_lengths)
    ended = doc_ends[None, :] <= position[:, None]
    doc_start = jnp.max(jnp.where(ended, doc_ends[None, :], 0), axis=1)
    low = jnp.maximum(position - (ATTEND_WINDOW - 1), doc_start) - ctx_index * tokens
    return jnp.broadcast_to(low[:, None], (tokens, 128))


def on_device(queries, rotated_key_rows, value_head_rows, w_out, post_gain, doc_lengths):
    tokens = queries.shape[0]
    heads = queries.shape[1] // HEAD_SIZE
    kv_heads = rotated_key_rows.shape[1] // HEAD_SIZE
    ctx_size, tp_size = lax.axis_size("ctx"), lax.axis_size("tp")
    tp_index = lax.axis_index("tp")
    rows = tokens // tp_size
    low = row_limits(lax.axis_index("ctx"), tokens, doc_lengths)

    near = (lax.axis_index("ctx") % 2).astype(jnp.int32)
    halos = []
    for head in range(kv_heads):
        cols = slice(head * HEAD_SIZE, (head + 1) * HEAD_SIZE)
        both = jnp.concatenate([rotated_key_rows[:, cols], value_head_rows[:, cols]], axis=1)
        chip = lax.ppermute(both, "ctx", [(i, i ^ 1) for i in range(ctx_size)])
        link = lax.ppermute(chip, "ctx", [(i, i + 2) for i in range(0, ctx_size - 2, 2)])
        halos.append((chip, link))

    attn = []
    for head in range(kv_heads):
        after = (halos[head], attn[-1]) if attn else halos[head]
        which = jnp.stack([near, jnp.int32(head)])
        attn.append(
            attend(which, tie(low, after), queries, rotated_key_rows, value_head_rows, halos[head], heads // kv_heads)
        )

    ring = ring_order(ctx_size)
    gathered, column = [], 0
    for chunks, width in CHUNKS:
        part = jnp.stack([w_out[:, :, column + i * width : column + (i + 1) * width] for i in range(chunks)])
        if len(gathered) == 1:
            part = tie(part, (attn[:-1], [link for _, link in halos]))
        gathered.append(lax.all_gather(part, "ctx", axis=0, tiled=False, axis_index_groups=[ring]))
        column += chunks * width

    kept, arrived = [], []
    starts = [(1 - tp_index) * rows, tp_index * rows] if tp_size == 2 else [jnp.int32(0)]
    where = jnp.stack([jnp.int32(i) for i in ring] + [i.astype(jnp.int32) for i in starts])
    for gather in gathered:
        for chunk in range(gather.shape[1]):
            number = len(kept)
            if number:
                where = tie(where, (kept[-1], arrived[number - 3] if number > 2 else ()))
            if tp_size == 2:
                send, keep = project(where, attn, gather, chunk, 2)
                arrived.append(lax.ppermute(send, "tp", [(0, 1), (1, 0)]))
            else:
                (keep,) = project(where, attn, gather, chunk, 1)
                if tp_size > 1:
                    keep = lax.psum_scatter(keep, "tp", scatter_dimension=0, tiled=True)
                arrived.append(jnp.zeros_like(keep))
            kept.append(keep)
    return sum_and_norm(kept, arrived, post_gain)


def solution(mesh):
    placed = (P("ctx", "tp"), P("ctx", "tp"), P("ctx", "tp"), P("tp", "ctx", None), P(), P())
    return jax.shard_map(
        on_device, mesh=mesh, in_specs=placed, out_specs=P(("ctx", "tp"), None), check_vma=False
    )
```
